32 devices in a mesh: row: 16 (over z, y, x), col: 2 (over core).
Axes of the slice: x: 2, y: 2, z: 4, core: 2. Of those that a mesh axis runs over, the one named last changes fastest.
Arguments:
- blocks: float32 [16, 2, 40, 128, 128], P('row', 'col'), may hold values from -0.078125 to 0.078125
- block_rows: int32 [16, 2, 40], P('row', 'col'), may hold values from 0 to 15
- block_cols: int32 [16, 2, 40], P(None, 'col'), may hold values from 0 to 127, as said below
- start_basis: float32 [32, 32768], P(None, ('row', 'col')), may hold values from -6 to 6
- targets: int32 [16], replicated, may hold values from 0 to 31, as said below
Outputs:
- right_basis: float32 [32, 32768], P(None, ('row', 'col'))
- left_basis: float32 [32, 32768], P(None, ('row', 'col'))
- triangle: float32 [32, 32], replicated
The draws below stay inside these ranges and needn't reach their ends.
Inputs may be any that keep to these rules, and one draw needn't show every extreme that they name: For every r, c and o < 16, all entries block_cols[r, c, n] with block_cols[r, c, n] // 8 = o are equal. `targets`: 16 distinct indices.
All inputs are finite; a program needn't handle non-finite values.
Results may differ from the reference program's by a relative error of at most 0.0001.
Values sent between devices are 32-bit elements; how exact they have to be, the bound alone decides.
No kernel may reach another device: no remote copies, remote signals or barrier semaphores. Data moves between devices by JAX's collectives and lax.ppermute only.
A program may use at most 64 MiB of HBM per device.

```python
import jax
import jax.numpy as jnp
from jax import lax

BLK = 128
SEGS = 8
K = 32
NT = 16
NNZ_DEV = 40
OUTER = 2
INNER = 4
NSEG = 256
NROWS = 32768
N_ROW = 16
N_COL = 2


def draw_targets(key, part):
    order = jax.random.permutation(key, K)
    return order[:NT].astype(jnp.int32)


def draw_block_cols(key, part):
    owner_key = jax.random.fold_in(key, 11)
    segment_key = jax.random.fold_in(key, 12)
    owners = jax.random.randint(owner_key, (N_ROW, N_COL, NNZ_DEV), 0, N_ROW)
    picks = jax.random.randint(segment_key, (N_ROW, N_COL, N_ROW), 0, SEGS)
    within = jnp.take_along_axis(picks, owners, axis=2)
    return (owners * SEGS + within).astype(jnp.int32)


def with_ends(result, rng, low, top_value):
    spot = [jax.random.randint(jax.random.fold_in(rng, axis), (), 0, length) for axis, length in enumerate(result.shape)]
    longest = result.shape.index(max(result.shape))
    next_to = spot[:longest] + [(spot[longest] + 1) % result.shape[longest]] + spot[longest + 1:]
    return result.at[tuple(spot)].set(low).at[tuple(next_to)].set(top_value)


def block_scale(rng, extent, pieces, low, top_value):
    level, own = 1.0, jax.random.fold_in(rng, 6)
    for axis_at, shards_of in pieces:
        steps = jnp.exp(jax.random.uniform(jax.random.fold_in(own, axis_at), (shards_of,), jnp.float32, low / len(pieces), top_value / len(pieces)))
        level = level * jnp.repeat(steps, extent[axis_at] // shards_of).reshape([-1 if axis == axis_at else 1 for axis in range(len(extent))])
    return level


def normal_values(rng, dims, spread, limit, shards=(), kind=jnp.bfloat16):
    drawn = spread * jax.random.normal(rng, dims, jnp.float32)
    if shards:
        drawn = drawn * block_scale(rng, dims, shards, -0.22, 0.18)
    return jnp.clip(drawn, -limit, limit).astype(kind)


def setup_inputs(seed: int = 0) -> dict:
    key_list = jax.random.split(jax.random.key(seed), 6)
    return {
        "blocks": normal_values(key_list[0], (N_ROW, N_COL, NNZ_DEV, BLK, BLK), (BLK * NNZ_DEV) ** -0.5, 0.078125, ((0, 16), (1, 2)), jnp.float32),
        "block_rows": with_ends(jax.random.randint(key_list[1], (N_ROW, N_COL, NNZ_DEV), 0, SEGS * N_COL), jax.random.fold_in(key_list[1], 1), 0, (SEGS * N_COL) - 1).astype(jnp.int32),
        "block_cols": draw_block_cols(jax.random.fold_in(key_list[5], 71), 0),
        "start_basis": normal_values(key_list[3], (K, NROWS), 1.0, 6.0, ((1, 32),), jnp.float32),
        "targets": draw_targets(jax.random.fold_in(key_list[5], 71), 0),
    }


highest = lax.Precision.HIGHEST

def lower_solve(lower, vectors):
    return lax.linalg.triangular_solve(lower, vectors, left_side=True, lower=True)

def lower_factor(vectors, total_rows):
    gram_sum = jnp.dot(vectors, vectors.T, precision=highest) / total_rows
    return jnp.linalg.cholesky(gram_sum)

def row_segments(block_rows):
    return jnp.arange(N_ROW, dtype=jnp.int32)[:, None, None] * (N_COL * SEGS) + block_rows

def col_segments(block_cols):
    col_ids = jnp.arange(N_COL, dtype=jnp.int32)
    owners = block_cols // SEGS
    within = block_cols % SEGS
    return ((owners * N_COL + col_ids[None, :, None]) * SEGS + within).astype(jnp.int32)

def apply_matrix(blocks, row_ids, col_ids_all, vectors):
    count_vectors = vectors.shape[0]
    block_size = blocks.shape[-1]
    segments = vectors.reshape(count_vectors, NSEG, block_size)

    def add_row(totals, row_index):
        picked = segments[:, col_ids_all[row_index]]
        products = jnp.einsum('cnij,kcnj->kcni', blocks[row_index], picked, precision=highest)
        totals = totals.at[:, row_ids[row_index].reshape(-1)].add(products.reshape(count_vectors, -1, block_size))
        return (totals, None)
    start_totals = jnp.zeros((count_vectors, NSEG, block_size), jnp.float32)
    totals, unused = lax.scan(add_row, start_totals, jnp.arange(N_ROW, dtype=jnp.int32))
    return totals.reshape(count_vectors, -1)

def apply_transpose(blocks, row_ids, col_ids_all, vectors):
    count_vectors = vectors.shape[0]
    block_size = blocks.shape[-1]
    segments = vectors.reshape(count_vectors, NSEG, block_size)

    def add_row(totals, row_index):
        picked = segments[:, row_ids[row_index]]
        products = jnp.einsum('cnij,kcni->kcnj', blocks[row_index], picked, precision=highest)
        totals = totals.at[:, col_ids_all[row_index].reshape(-1)].add(products.reshape(count_vectors, -1, block_size))
        return (totals, None)
    start_totals = jnp.zeros((count_vectors, NSEG, block_size), jnp.float32)
    totals, unused = lax.scan(add_row, start_totals, jnp.arange(N_ROW, dtype=jnp.int32))
    return totals.reshape(count_vectors, -1)

def column_squares(blocks, col_ids_all):
    block_size = blocks.shape[-1]

    def add_row(totals, row_index):
        block_tiles = blocks[row_index]
        squared = jnp.sum(block_tiles * block_tiles, axis=2)
        return (totals.at[col_ids_all[row_index].reshape(-1)].add(squared.reshape(-1, block_size)), None)
    start_totals = jnp.zeros((NSEG, block_size), jnp.float32)
    totals, unused = lax.scan(add_row, start_totals, jnp.arange(N_ROW, dtype=jnp.int32))
    return totals.reshape(-1)

def reference(blocks, block_rows, block_cols, start_basis, targets):
    block_size = blocks.shape[-1]
    total_rows = float(block_size * NSEG)
    count_vectors = start_basis.shape[0]
    row_ids = row_segments(block_rows)
    col_ids_all = col_segments(block_cols)
    squares = column_squares(blocks, col_ids_all)
    largest = jnp.max(squares)
    chosen = jnp.sum((targets[None, :] == jnp.arange(count_vectors, dtype=jnp.int32)[:, None]).astype(jnp.float32), axis=1)
    trial_basis = start_basis
    left_basis = start_basis
    lower_image = jnp.zeros((count_vectors, count_vectors), jnp.float32)
    for outer_step in range(OUTER):
        lower_basis = lower_factor(trial_basis, total_rows)
        right_now = lower_solve(lower_basis, trial_basis)
        image = apply_matrix(blocks, row_ids, col_ids_all, right_now)
        lower_image = lower_factor(image, total_rows)
        left_basis = lower_solve(lower_image, image)
        back = apply_transpose(blocks, row_ids, col_ids_all, left_basis)
        residual = back - jnp.dot(lower_image.T, right_now, precision=highest)
        shifts = jnp.sum(lower_image * lower_image, axis=1) + largest
        correction = jnp.zeros_like(residual)
        for inner_step in range(INNER):
            coupling = jnp.dot(right_now, (squares[None, :] * correction).T, precision=highest) / total_rows
            correction = (residual + squares[None, :] * correction - jnp.dot(coupling.T, right_now, precision=highest)) / shifts[:, None]
        trial_basis = right_now + chosen[:, None] * correction
    lower_basis = lower_factor(trial_basis, total_rows)
    return (lower_solve(lower_basis, trial_basis), left_basis, lower_image.T)
```

```python
import jax
import jax.numpy as jnp
from jax import lax
from jax.sharding import PartitionSpec as P

OUTER = 2
INNER = 4

highest = lax.Precision.HIGHEST


def mm(a, b):
    return jnp.dot(a, b, precision=highest)


def gram(a, b):
    return lax.dot_general(a, b, (((1,), (1,)), ((), ())), precision=highest)


def axis_exchange(x, axis, mask):
    count = lax.axis_size(axis)
    return lax.ppermute(x, axis, [(i, i ^ mask) for i in range(count)])


def axis_sum(x, axis):
    count = lax.axis_size(axis)
    if count & (count - 1):
        return lax.psum(x, axis)
    bit = 1
    while bit < count:
        masks = (bit, 2 * bit, 3 * bit) if 2 * bit < count else (bit,)
        x = x + sum(axis_exchange(x, axis, mask) for mask in masks)
        bit *= 4
    return x


def exchange(x):
    return lax.all_to_all(x, "row", split_axis=0, concat_axis=0, tiled=True)


def lower_inverse(lower):
    eye = jnp.eye(lower.shape[0], dtype=lower.dtype)
    return lax.linalg.triangular_solve(lower, eye, left_side=True, lower=True)


def correct(factors, largest, chosen, cols_v, cols_w, cols_s):
    lower_inv, lower_image, image_inv, scale, couplings = factors
    basis = mm(lower_inv, cols_v)
    residual = mm(mm(image_inv, lower_inv), cols_w) - mm(lower_image.T, basis)
    correction = scale * residual
    for coupling in couplings:
        correction = scale * (residual + cols_s * correction - mm(coupling.T, basis))
    return basis + (chosen / largest) * correction


def factor(gram_v, gram_y, total_rows, largest):
    lower = jnp.linalg.cholesky(gram_v / total_rows)
    lower_inv = lower_inverse(lower)
    gram_image = mm(mm(lower_inv, gram_y / total_rows), lower_inv.T)
    lower_image = jnp.linalg.cholesky(gram_image)
    image_inv = lower_inverse(lower_image)
    scale = largest / (jnp.sum(lower_image * lower_image, axis=1) + largest)
    return lower_inv, lower_image, image_inv, scale


def couple(facts, moments_vv, moments_vw, total_rows):
    lower_inv, lower_image, image_inv, scale = facts
    to_image = mm(image_inv, lower_inv)
    bb = [mm(mm(lower_inv, m / total_rows), lower_inv.T) for m in moments_vv]
    br = [
        mm(mm(lower_inv, m / total_rows), to_image.T) - mm(b, lower_image)
        for m, b in zip(moments_vw, bb)
    ]
    couplings = []
    powers = [scale[None, :] ** (k + 1) for k in range(INNER)]
    for m in range(INNER - 1):
        value = sum(br[k] * powers[k] for k in range(m + 1))
        for k in range(m):
            value = value - mm(bb[k], couplings[m - 1 - k]) * powers[k]
        couplings.append(value)
    return lower_inv, lower_image, image_inv, scale[:, None], couplings


def shards(blocks, block_rows, block_cols, start_basis, targets):
    size = blocks.shape[-1]
    tiles = blocks.reshape(-1, size, size)
    rows_local = block_rows.reshape(-1)
    row_count = lax.axis_size("row")
    col_count = lax.axis_size("col")
    width = start_basis.shape[1]
    seg_count = width // size
    total_rows = float(width * row_count * col_count)
    vectors = start_basis.shape[0]
    pattern = block_cols[:, 0, :]
    me_row = lax.axis_index("row")
    me_col = lax.axis_index("col")
    cols_local = lax.dynamic_index_in_dim(pattern, me_row, 0, keepdims=False)
    owners = cols_local // seg_count
    seg_ids = jnp.arange(seg_count, dtype=jnp.int32)
    matched = pattern // seg_count == me_row
    within = pattern % seg_count
    pick_hot = jnp.any(
        matched[:, :, None] & (within[:, :, None] == seg_ids[None, None, :]), axis=1
    ).astype(jnp.float32)
    owner_hot = (owners[:, None] == jnp.arange(row_count, dtype=jnp.int32)[None, :]).astype(
        jnp.float32
    )
    row_hot = (
        rows_local[:, None] == jnp.arange(col_count * seg_count, dtype=jnp.int32)[None, :]
    ).astype(jnp.float32)
    chosen = jnp.sum(
        (targets[None, :] == jnp.arange(vectors, dtype=jnp.int32)[:, None]).astype(jnp.float32),
        axis=1,
    )[:, None]

    def to_tiles(cols):
        segs = cols.reshape(cols.shape[0], seg_count, size)
        return jnp.einsum("rt,ktb->rkb", pick_hot, segs, precision=highest)

    def from_tiles(parts):
        cols = jnp.einsum("rt,rkb->ktb", pick_hot, parts, precision=highest)
        return cols.reshape(cols.shape[0], -1)

    def apply(parts):
        picked = parts[owners]
        products = jnp.einsum("nij,nkj->kni", tiles, picked, precision=highest)
        return jnp.einsum("nr,kni->kri", row_hot, products, precision=highest).reshape(
            parts.shape[1], -1
        )

    def apply_back(image):
        segs = image.reshape(image.shape[0], -1, size)
        products = jnp.einsum("nij,kni->knj", tiles, segs[:, rows_local], precision=highest)
        return jnp.einsum("no,knj->okj", owner_hot, products, precision=highest)

    def spread(rows):
        return jnp.broadcast_to(rows[None], (row_count,) + rows.shape)

    own_v = start_basis
    squared = jnp.sum(tiles * tiles, axis=1)
    square_parts = jnp.einsum("no,nj->oj", owner_hot, squared, precision=highest)
    got = exchange(jnp.concatenate([to_tiles(own_v), square_parts[:, None, :]], axis=1))
    tile_v, square_parts = got[:, :vectors], got[:, vectors:]
    squares = from_tiles(square_parts)
    image_part = apply(tile_v)
    gram_v = gram(own_v, own_v)
    slots = jnp.where(jnp.arange(col_count) == me_col, jnp.max(squares), 0.0)
    slots = jnp.broadcast_to(slots, (vectors, col_count))
    summed = axis_sum(jnp.concatenate([image_part, gram_v, slots], axis=1), "col")
    span = image_part.shape[1]
    image, gram_v = summed[:, :span], summed[:, span : span + vectors]
    top = jnp.max(summed[:, span + vectors :])
    gram_y = gram(image, image)
    top = jnp.broadcast_to(top, (vectors, size - 2 * vectors))
    extra = jnp.concatenate([gram_v, gram_y, top], axis=1)
    got = exchange(jnp.concatenate([apply_back(image), spread(extra)], axis=1))
    own_w = from_tiles(got[:, :vectors])
    extra = jnp.sum(got[:, vectors:, : 2 * vectors], axis=0)
    gram_v, gram_y = extra[:, :vectors], extra[:, vectors:]
    largest = jnp.max(got[:, vectors, 2 * vectors])
    own_s = squares / largest
    moments = []
    power = own_v
    for _ in range(INNER - 1):
        power = power * own_s
        moments += [gram(power, own_v), gram(power, own_w)]
    send = jnp.concatenate([to_tiles(own_w), to_tiles(own_s)], axis=1)
    got = exchange(send)
    moments = axis_sum(axis_sum(jnp.concatenate(moments, axis=1), "col"), "row")
    tile_w, tile_s = got[:, :vectors], got[:, vectors:]
    facts = factor(gram_v, gram_y, total_rows, largest)
    moments = jnp.split(moments, 2 * (INNER - 1), axis=1)
    factors = couple(facts, moments[0::2], moments[1::2], total_rows)

    def flat(parts):
        return jnp.swapaxes(parts, 0, 1).reshape(parts.shape[1], -1)

    def unflat(cols):
        return jnp.swapaxes(cols.reshape(cols.shape[0], -1, size), 0, 1)

    own_v, own_v_old = correct(factors, largest, chosen, own_v, own_w, own_s), own_v
    tile_v = unflat(correct(factors, largest, chosen, flat(tile_v), flat(tile_w), flat(tile_s)))

    powers = [tile_v]
    for _ in range(INNER - 1):
        powers.append(powers[-1] * tile_s)
    image_part = apply(jnp.concatenate(powers, axis=1))
    image_part = image_part.reshape(INNER, vectors, -1)
    image_part = jnp.concatenate(list(image_part), axis=1)
    moments = [gram(own_v, own_v)]
    power = own_v
    for _ in range(INNER - 1):
        power = power * own_s
        moments.append(gram(power, own_v))
    summed = axis_sum(jnp.concatenate([image_part] + moments, axis=1), "col")
    span = image_part.shape[1] // INNER
    image = summed[:, :span]
    moments_v = summed[:, INNER * span :]
    images = [summed[:, k * span : (k + 1) * span] for k in range(INNER)]
    moments_y = [gram(z, image) for z in images]
    extra = jnp.concatenate([moments_v] + moments_y, axis=1)
    extra = axis_sum(extra, "row")
    got = exchange(apply_back(image))
    own_w = from_tiles(got)
    parts = jnp.split(extra, 2 * INNER, axis=1)
    gram_v, moments_vv = parts[0], parts[1:INNER]
    gram_y, moments_vw = parts[INNER], parts[INNER + 1 :]
    facts = factor(gram_v, gram_y, total_rows, largest)
    factors = couple(facts, moments_vv, moments_vw, total_rows)
    trial = correct(factors, largest, chosen, own_v, own_w, own_s)
    gram_t = axis_sum(gram(trial, trial), "col")
    gram_t = jnp.sum(exchange(spread(gram_t)), axis=0)
    right = mm(lower_inverse(jnp.linalg.cholesky(gram_t / total_rows)), trial)
    lower_inv, lower_image, image_inv = facts[:3]
    image_own = lax.dynamic_slice_in_dim(image, me_col * width, width, axis=1)
    left = mm(mm(image_inv, lower_inv), image_own)
    return right, left, lower_image.T


def solution(mesh):
    in_specs = (
        P("row", "col", None, None, None),
        P("row", "col", None),
        P(None, "col", None),
        P(None, ("row", "col")),
        P(),
    )
    out_specs = (P(None, ("row", "col")), P(None, ("row", "col")), P())
    return jax.shard_map(shards, mesh=mesh, in_specs=in_specs, out_specs=out_specs, check_vma=False)
```

```python
import functools

import jax
import jax.numpy as jnp
from jax import lax
from jax.experimental import pallas as pl
from jax.experimental.pallas import tpu as pltpu
from jax.sharding import PartitionSpec as P

OUTER = 2
INNER = 4
PAD = 8

highest = lax.Precision.HIGHEST
f32 = jnp.float32


def mm(a, b):
    return lax.dot_general(a, b, (((1,), (0,)), ((), ())), precision=highest, preferred_element_type=f32)


def mt(a, b):
    return lax.dot_general(a, b, (((1,), (1,)), ((), ())), precision=highest, preferred_element_type=f32)


def lanes(values):
    return jnp.concatenate(values, axis=1)


def column(row):
    count = row.shape[1]
    eye = lax.broadcasted_iota(jnp.int32, (count, count), 0) == lax.broadcasted_iota(
        jnp.int32, (count, count), 1
    )
    return jnp.sum(jnp.where(eye, row, 0.0), axis=1, keepdims=True)


def axis_parts(x, axis):
    count = lax.axis_size(axis)
    if count & (count - 1):
        return [lax.psum(x, axis)]
    parts = [x]
    bit = 1
    while bit < count:
        if len(parts) > 1:
            x = functools.reduce(jnp.add, parts)
        masks = (bit, 2 * bit, 3 * bit) if 2 * bit < count else (bit,)
        parts = [x] + [
            lax.ppermute(x, axis, [(i, i ^ mask) for i in range(count)]) for mask in masks
        ]
        bit *= 4
    return parts


def axis_sum(x, axis):
    return functools.reduce(jnp.add, axis_parts(x, axis))


def exchange(x):
    return lax.all_to_all(x, "row", split_axis=0, concat_axis=0, tiled=True)


smem = pl.BlockSpec(memory_space=pltpu.SMEM)
vmem = pl.BlockSpec(memory_space=pltpu.VMEM)


def call(kernel, outs, args, scratch=(), name=None):
    specs = [smem if jnp.issubdtype(a.dtype, jnp.integer) else vmem for a in args]
    return pl.pallas_call(
        kernel,
        out_shape=tuple(jax.ShapeDtypeStruct(s, f32) for s in outs),
        in_specs=specs,
        out_specs=tuple(vmem for _ in outs),
        scratch_shapes=list(scratch),
        compiler_params=pltpu.CompilerParams(vmem_limit_bytes=32 << 20),
        name=name,
    )(*args)


def seg_slice(index, size):
    return pl.ds(pl.multiple_of(index * size, size), size)


def factor_inverse(gram_sum):
    count = gram_sum.shape[0]
    rows = lax.broadcasted_iota(jnp.int32, (count, count), 0)
    cols = lax.broadcasted_iota(jnp.int32, (count, count), 1)
    state = lanes([gram_sum, jnp.where(rows == cols, 1.0, 0.0)])
    below = lax.broadcasted_iota(jnp.int32, (count, 1), 0)
    for k in range(count):
        pivot_row = state[k : k + 1, :]
        scaled = pivot_row / state[k : k + 1, k : k + 1]
        factor = jnp.where(below > k, state[:, k : k + 1], 0.0)
        state = state - factor * scaled
    left = state[:, :count]
    diag = jnp.sum(jnp.where(rows == cols, left, 0.0), axis=1, keepdims=True)
    state = state * (1.0 / jnp.sqrt(diag))
    return jnp.where(cols >= rows, state[:, :count], 0.0), state[:, count:]


def factor(gram_v, gram_y, top, total_rows):
    unused, lower_inv = factor_inverse(gram_v / total_rows)
    gram_image = mt(mm(lower_inv, gram_y / total_rows), lower_inv)
    upper, image_inv = factor_inverse(gram_image)
    sums = jnp.sum(upper * upper, axis=0, keepdims=True)
    scale = column(top / (sums + top))
    return lower_inv, upper, mm(image_inv, lower_inv), scale


def couple(facts, moments_vv, moments_wv, total_rows):
    lower_inv, upper, to_left, scale = facts
    bb = [mt(mm(lower_inv, m / total_rows), lower_inv) for m in moments_vv]
    rb = [
        mt(mm(to_left, m / total_rows), lower_inv) - mm(upper, b)
        for m, b in zip(moments_wv, bb)
    ]
    powers = [scale]
    for _ in range(INNER - 2):
        powers.append(powers[-1] * scale)
    couplings = []
    base = 0.0
    for m in range(INNER - 1):
        base = base + powers[m] * rb[m]
        value = base
        for k in range(m):
            value = value - powers[k] * mm(couplings[m - 1 - k], bb[k])
        couplings.append(value)
    on_basis = [lower_inv, -mm(upper, lower_inv)] + [mm(c, lower_inv) for c in couplings]
    return jnp.concatenate(on_basis, axis=0)


def correct(on_basis, to_left, scale, gain, cols_v, cols_w, cols_s):
    count = to_left.shape[0]
    mixed = mm(on_basis, cols_v)
    part = lambda k: mixed[k * count : (k + 1) * count]
    basis = part(0)
    residual = part(1) + mm(to_left, cols_w)
    correction = scale * residual
    for m in range(INNER - 1):
        correction = scale * (residual + cols_s * correction - part(2 + m))
    return basis + gain * correction


def selected(targets, count):
    rows = lax.broadcasted_iota(jnp.int32, (count, 1), 0)
    chosen = jnp.zeros((count, 1), f32)
    for t in range(targets.shape[0]):
        chosen = chosen + jnp.where(rows == targets[t], 1.0, 0.0)
    return chosen


def apply_tiles(tiles, rows, owners, source, image, size):
    count = tiles.shape[0]
    image[...] = jnp.zeros_like(image)

    def step(n, carry):
        at = seg_slice(rows[n], size)
        image[:, at] += mt(source(owners[n]), tiles[n])
        return carry

    lax.fori_loop(0, count, step, 0, unroll=8)


def apply_back(tiles, rows, owners, image, send, vectors, size):
    count = tiles.shape[0]

    def step(n, carry):
        picked = image[:vectors, seg_slice(rows[n], size)]
        send[owners[n], :vectors, :] += mm(picked, tiles[n])
        return carry

    lax.fori_loop(0, count, step, 0, unroll=8)


def pack_kernel(tiles, vectors, segs, owners, send):
    size = tiles.shape[-1]
    count = vectors.shape[0]
    send[:, count:, :] = jnp.zeros((send.shape[0], PAD, size), f32)
    for r in range(send.shape[0]):
        send[r, :count, :] = vectors[:, seg_slice(segs[r], size)]

    def step(n, carry):
        tile = tiles[n]
        send[owners[n], count : count + 1, :] += jnp.sum(tile * tile, axis=0, keepdims=True)
        return carry

    lax.fori_loop(0, tiles.shape[0], step, 0, unroll=8)


def first_kernel(slot, tiles, got, vectors, segs, rows, owners, image, squares):
    size = tiles.shape[-1]
    count = vectors.shape[0]
    span = image.shape[1] - size
    squares[...] = jnp.zeros_like(squares)
    for r in range(got.shape[0]):
        squares[:, seg_slice(segs[r], size)] += got[r, count : count + PAD, :]
    apply_tiles(tiles, rows, owners, lambda o: got[o, :count, :], image, size)
    image[:, span:] = jnp.zeros((count, size), f32)
    image[:, span : span + count] = mt(vectors[...], vectors[...])
    where = lax.broadcasted_iota(jnp.int32, (count, size - count), 1) == slot[0]
    image[:, span + count :] = jnp.where(where, jnp.max(squares[...]), 0.0)


def first_back_kernel(parts_count, tiles, rows, owners, *refs):
    parts, send, image = refs[:parts_count], refs[-2], refs[-1]
    size = tiles.shape[-1]
    count = image.shape[0]
    span = image.shape[1] - size
    image[...] = functools.reduce(jnp.add, [p[...] for p in parts])
    top = jnp.max(image[:, span + count :])
    summed = image[:, :span]
    gram_y = mt(summed, summed)
    gram_v = image[:, span : span + count]
    half = count // 2
    extra = lanes(
        [gram_v[:half], gram_v[half:], gram_y[:half], gram_y[half:]]
    )
    send[:, :count, :] = jnp.zeros((send.shape[0], count, size), f32)
    for r in range(send.shape[0]):
        send[r, count : count + half, :] = extra
        send[r, count + half :, :] = jnp.broadcast_to(top, (PAD, size))
    apply_back(tiles, rows, owners, image, send, count, size)


def powers_of(values, scales):
    powers = [values]
    for _ in range(INNER - 1):
        powers.append(powers[-1] * scales)
    return powers


def gather_cols(got, segs, cols, count, size):
    cols[...] = jnp.zeros_like(cols)
    for r in range(got.shape[0]):
        cols[:, seg_slice(segs[r], size)] += got[r, :count, :]


def moment_kernel(got, vectors, squares, segs, send, moments, small, own_w, own_s):
    count = vectors.shape[0]
    size = got.shape[-1]
    half = count // 2
    gather_cols(got, segs, own_w, count, size)
    extra = got[0, count : count + half, :]
    top = got[0, count + half :, :]
    for r in range(1, got.shape[0]):
        extra = extra + got[r, count : count + half, :]
        top = jnp.maximum(top, got[r, count + half :, :])
    largest = jnp.max(top)
    own_s[...] = squares[...] / largest
    small[...] = jnp.zeros_like(small)
    small[:half, :count] = extra[:, :count]
    small[half:, :count] = extra[:, count : 2 * count]
    small[:half, count : 2 * count] = extra[:, 2 * count : 3 * count]
    small[half:, count : 2 * count] = extra[:, 3 * count : 4 * count]
    small[:, 2 * count :] = jnp.broadcast_to(largest, (count, size - 2 * count))
    for r in range(send.shape[0]):
        at = seg_slice(segs[r], size)
        send[r, :count, :] = own_w[:, at]
        send[r, count:, :] = own_s[:, at]
    values = vectors[...]
    both = jnp.concatenate([values, own_w[...]], axis=0)
    scales = own_s[0:1, :]
    moments[...] = jnp.zeros_like(moments)
    for j in range(1, INNER):
        values = values * scales
        found = mt(both, values)
        moments[:, (j - 1) * count : j * count] = found[:count]
        moments[:, size + (j - 1) * count : size + j * count] = found[count:]


def factor_kernel(total_rows, small, facts):
    count = small.shape[0]
    lower_inv, upper, to_left, scale = factor(
        small[:, :count],
        small[:, count : 2 * count],
        small[0:1, 2 * count : 2 * count + 1],
        total_rows,
    )
    facts[0] = lower_inv
    facts[1] = upper
    facts[2] = to_left
    facts[3] = jnp.broadcast_to(scale, (count, count))


def second_kernel(
    total_rows, parts_count, tiles, got_v, got, vectors, own_w, own_s, small, facts,
    targets, rows, owners, *refs
):
    parts = refs[:parts_count]
    image, own_next, powers = refs[parts_count:]
    count = vectors.shape[0]
    size = tiles.shape[-1]
    span = image.shape[1] - size
    moments = functools.reduce(jnp.add, [p[...] for p in parts])
    moments_vv = [moments[:, k * count : (k + 1) * count] for k in range(INNER - 1)]
    moments_wv = [moments[:, size + k * count : size + (k + 1) * count] for k in range(INNER - 1)]
    to_left, scale = facts[2], facts[3][:, 0:1]
    on_basis = couple((facts[0], facts[1], to_left, scale), moments_vv, moments_wv, total_rows)
    gain = selected(targets, count) / small[:, 2 * count : 2 * count + 1]
    tile_v = lanes([got_v[r, :count, :] for r in range(got.shape[0])])
    tile_w = lanes([got[r, :count, :] for r in range(got.shape[0])])
    tile_s = lanes([got[r, count : count + 1, :] for r in range(got.shape[0])])
    tile_v = correct(on_basis, to_left, scale, gain, tile_v, tile_w, tile_s)
    for k in range(INNER):
        for r in range(got.shape[0]):
            powers[r, k * count : (k + 1) * count, :] = tile_v[:, r * size : (r + 1) * size]
        if k + 1 < INNER:
            tile_v = tile_v * tile_s
    own = correct(on_basis, to_left, scale, gain, vectors[...], own_w[...], own_s[0:1, :])
    own_next[...] = own
    apply_tiles(tiles, rows, owners, lambda o: powers[o], image, size)
    image[count:, span:] = jnp.zeros((image.shape[0] - count, size), f32)
    values = own
    for k in range(INNER):
        image[:count, span + k * count : span + (k + 1) * count] = mt(own, values)
        values = values * own_s[0:1, :]


def second_back_kernel(parts_count, tiles, rows, owners, *refs):
    parts, (send, moments, image) = refs[:parts_count], refs[parts_count:]
    size = tiles.shape[-1]
    count = image.shape[0]
    span = image.shape[1]
    image[...] = functools.reduce(jnp.add, [p[:count, :span] for p in parts])
    moments[:, :size] = functools.reduce(jnp.add, [p[:count, span:] for p in parts])
    summed = image[...]
    others = functools.reduce(jnp.add, [p[:, :span] for p in parts])
    found = mt(summed, others)
    moments[:, size:] = found
    send[...] = jnp.zeros_like(send)
    apply_back(tiles, rows, owners, image, send, count, size)


def second_factor_kernel(total_rows, parts_count, small, *refs):
    parts, (facts, on_basis) = refs[:parts_count], refs[parts_count:]
    count = small.shape[0]
    size = small.shape[1]
    moments = functools.reduce(jnp.add, [p[...] for p in parts])
    pick = lambda k: moments[:, k * count : (k + 1) * count]
    found = factor(pick(0), pick(INNER), small[0:1, 2 * count : 2 * count + 1], total_rows)
    facts[0] = found[0]
    facts[1] = found[1]
    facts[2] = found[2]
    facts[3] = jnp.broadcast_to(found[3], (count, count))
    on_basis[...] = couple(
        found,
        [pick(k) for k in range(1, INNER)],
        [pick(INNER + k) for k in range(1, INNER)],
        total_rows,
    )


def trial_kernel(got, vectors, own_s, small, facts, on_basis, segs, targets, trial, gram_part, own_w):
    count = vectors.shape[0]
    size = got.shape[-1]
    gather_cols(got, segs, own_w, count, size)
    gain = selected(targets, count) / small[:, 2 * count : 2 * count + 1]
    found = correct(
        on_basis[...], facts[2], facts[3][:, 0:1], gain, vectors[...], own_w[...], own_s[0:1, :]
    )
    trial[...] = found
    gram_sum = mt(found, found)
    rows = gram_part.shape[0]
    gram_part[...] = lanes([gram_sum[k * rows : (k + 1) * rows] for k in range(count // rows)])


def last_kernel(total_rows, got, trial, image, facts, right, left):
    count = trial.shape[0]
    packed = got[0]
    for r in range(1, got.shape[0]):
        packed = packed + got[r]
    gram_sum = jnp.concatenate(
        [packed[:, k * count : (k + 1) * count] for k in range(packed.shape[1] // count)], axis=0
    )
    left[...] = mm(facts[2], image[...])
    unused, lower_inv = factor_inverse(gram_sum / total_rows)
    right[...] = mm(lower_inv, trial[...])


def shards(blocks, block_rows, block_cols, start_basis, targets):
    size = blocks.shape[-1]
    tiles = blocks.reshape(-1, size, size)
    rows = block_rows.reshape(-1)
    row_count = lax.axis_size("row")
    col_count = lax.axis_size("col")
    count, width = start_basis.shape
    seg_count = width // size
    span = col_count * width
    total_rows = float(width * row_count * col_count)
    pattern = block_cols[:, 0, :]
    me_row = lax.axis_index("row")
    me_col = lax.axis_index("col")
    owners = lax.dynamic_index_in_dim(pattern, me_row, 0, keepdims=False) // seg_count
    segs = jnp.max(
        jnp.where(pattern // seg_count == me_row, pattern % seg_count, 0), axis=1
    )
    slot = me_col.reshape(1)

    (send,) = call(
        pack_kernel, [(row_count, count + PAD, size)], [tiles, start_basis, segs, owners], name="pack"
    )
    got_v = exchange(send)
    part, squares = call(
        first_kernel,
        [(count, span + size), (PAD, width)],
        [slot, tiles, got_v, start_basis, segs, rows, owners],
        name="first",
    )
    parts = axis_parts(part, "col")
    (send,) = call(
        functools.partial(first_back_kernel, len(parts)),
        [(row_count, count + count // 2 + PAD, size)],
        [tiles, rows, owners] + parts,
        scratch=[pltpu.VMEM((count, span + size), f32)],
        name="first_back",
    )
    got = exchange(send)
    send, moments, small, own_w, own_s = call(
        moment_kernel,
        [
            (row_count, count + PAD, size),
            (count, 2 * size),
            (count, size),
            (count, width),
            (PAD, width),
        ],
        [got, start_basis, squares, segs],
        name="moments",
    )
    got = exchange(send)
    parts = axis_parts(axis_sum(moments, "col"), "row")
    (facts,) = call(
        functools.partial(factor_kernel, total_rows), [(4, count, count)], [small], name="factor"
    )
    part, own_v = call(
        functools.partial(second_kernel, total_rows, len(parts)),
        [(INNER * count, span + size), (count, width)],
        [tiles, got_v, got, start_basis, own_w, own_s, small, facts, targets, rows, owners] + parts,
        scratch=[pltpu.VMEM((row_count, INNER * count, size), f32)],
        name="second",
    )
    parts = axis_parts(part, "col")
    send, moments, image = call(
        functools.partial(second_back_kernel, len(parts)),
        [(row_count, count, size), (count, 2 * size), (count, span)],
        [tiles, rows, owners] + parts,
        name="second_back",
    )
    got = exchange(send)
    parts = axis_parts(moments, "row")
    facts, on_basis = call(
        functools.partial(second_factor_kernel, total_rows, len(parts)),
        [(4, count, count), ((INNER + 1) * count, count)],
        [small] + parts,
        name="second_factor",
    )
    trial, gram_part = call(
        trial_kernel,
        [(count, width), (count * count // size, size)],
        [got, own_v, own_s, small, facts, on_basis, segs, targets],
        scratch=[pltpu.VMEM((count, width), f32)],
        name="trial",
    )
    gram_part = axis_sum(gram_part, "col")
    got = exchange(jnp.broadcast_to(gram_part[None], (row_count,) + gram_part.shape))
    image_own = lax.dynamic_slice_in_dim(image, me_col * width, width, axis=1)
    right, left = call(
        functools.partial(last_kernel, total_rows),
        [(count, width), (count, width)],
        [got, trial, image_own, facts],
        name="last",
    )
    return right, left, facts[1]


def solution(mesh):
    in_specs = (
        P("row", "col", None, None, None),
        P("row", "col", None),
        P(None, "col", None),
        P(None, ("row", "col")),
        P(),
    )
    out_specs = (P(None, ("row", "col")), P(None, ("row", "col")), P())
    return jax.shard_map(shards, mesh=mesh, in_specs=in_specs, out_specs=out_specs, check_vma=False)
```

```python
import functools

import jax
import jax.numpy as jnp
from jax import lax
from jax.experimental import pallas as pl
from jax.experimental.pallas import tpu as pltpu
from jax.sharding import PartitionSpec as P

OUTER = 2
INNER = 4
PAD = 8

highest = lax.Precision.HIGHEST
f32 = jnp.float32


def mm(a, b):
    return lax.dot_general(a, b, (((1,), (0,)), ((), ())), precision=highest, preferred_element_type=f32)


def mt(a, b):
    return lax.dot_general(a, b, (((1,), (1,)), ((), ())), precision=highest, preferred_element_type=f32)


def halves(x):
    high = x.astype(jnp.bfloat16)
    return high, (x - high.astype(f32)).astype(jnp.bfloat16)


def mm3(a, b):
    count = a.shape[0]
    a_high, a_low = halves(a)
    b_high, b_low = halves(b)
    dot = functools.partial(jnp.dot, preferred_element_type=f32)
    both = dot(jnp.concatenate([a_high, a_low], axis=0), b_high)
    return both[:count] + both[count:] + dot(a_high, b_low)


def lanes(values):
    return jnp.concatenate(values, axis=1)


def column(row):
    count = row.shape[1]
    eye = lax.broadcasted_iota(jnp.int32, (count, count), 0) == lax.broadcasted_iota(
        jnp.int32, (count, count), 1
    )
    return jnp.sum(jnp.where(eye, row, 0.0), axis=1, keepdims=True)


smem = pl.BlockSpec(memory_space=pltpu.SMEM)
vmem = pl.BlockSpec(memory_space=pltpu.VMEM)


def call(kernel, outs, args, scratch=(), name=None):
    specs = [smem if jnp.issubdtype(a.dtype, jnp.integer) else vmem for a in args]
    return pl.pallas_call(
        kernel,
        out_shape=tuple(jax.ShapeDtypeStruct(s, f32) for s in outs),
        in_specs=specs,
        out_specs=tuple(vmem for _ in outs),
        scratch_shapes=list(scratch),
        compiler_params=pltpu.CompilerParams(vmem_limit_bytes=12 << 20),
        name=name,
    )(*args)


def add_kernel(*refs):
    refs[-1][...] = functools.reduce(jnp.add, [p[...] for p in refs[:-1]])


def add(parts):
    if len(parts) == 1:
        return parts[0]
    return call(add_kernel, [parts[0].shape], parts, name="add")[0]


def axis_parts(x, axis):
    count = lax.axis_size(axis)
    if count & (count - 1):
        return [lax.psum(x, axis)]
    parts = [x]
    bit = 1
    while bit < count:
        x = add(parts)
        masks = (bit, 2 * bit, 3 * bit) if 2 * bit < count else (bit,)
        parts = [x] + [
            lax.ppermute(x, axis, [(i, i ^ mask) for i in range(count)]) for mask in masks
        ]
        bit *= 4
    return parts


def exchange(x, axes="row"):
    return lax.all_to_all(x, axes, split_axis=0, concat_axis=0, tiled=True)


def seg_slice(index, size):
    return pl.ds(pl.multiple_of(index * size, size), size)


def factor_inverse(gram_sum):
    count = gram_sum.shape[0]
    rows = lax.broadcasted_iota(jnp.int32, (count, count), 0)
    cols = lax.broadcasted_iota(jnp.int32, (count, count), 1)
    state = lanes([gram_sum, jnp.where(rows == cols, 1.0, 0.0)])
    below = lax.broadcasted_iota(jnp.int32, state.shape, 0)
    spread_col = lambda k: jnp.broadcast_to(state[:, k : k + 1], state.shape)
    current = spread_col(0)
    for k in range(count):
        ahead = spread_col(k + 1) if k + 1 < count else None
        factor = jnp.where(below > k, current, 0.0) * (1.0 / current[k : k + 1, :])
        if ahead is not None:
            ahead = ahead - factor * current[k + 1 : k + 2, :]
        state = state - factor * state[k : k + 1, :]
        current = ahead
    left = state[:, :count]
    diag = jnp.sum(jnp.where(rows == cols, left, 0.0), axis=1, keepdims=True)
    state = state * (1.0 / jnp.sqrt(diag))
    return jnp.where(cols >= rows, state[:, :count], 0.0), state[:, count:]


def factor(lower_inv, gram_y, top, total_rows):
    gram_image = mt(mm(lower_inv, gram_y / total_rows), lower_inv)
    upper, image_inv = factor_inverse(gram_image)
    sums = jnp.sum(upper * upper, axis=0, keepdims=True)
    scale = column(top / (sums + top))
    return lower_inv, upper, mm(image_inv, lower_inv), scale


def couple(facts, moments_vv, moments_wv, total_rows):
    lower_inv, upper, to_left, scale = facts
    bb = [mt(mm(lower_inv, m / total_rows), lower_inv) for m in moments_vv]
    rb = [
        mt(mm(to_left, m / total_rows), lower_inv) - mm(upper, b)
        for m, b in zip(moments_wv, bb)
    ]
    powers = [scale]
    for _ in range(INNER - 2):
        powers.append(powers[-1] * scale)
    couplings = []
    base = 0.0
    for m in range(INNER - 1):
        base = base + powers[m] * rb[m]
        value = base
        for k in range(m):
            value = value - powers[k] * mm(couplings[m - 1 - k], bb[k])
        couplings.append(value)
    on_basis = [lower_inv, -mm(upper, lower_inv)] + [mm(c, lower_inv) for c in couplings]
    return jnp.concatenate(on_basis, axis=0)


def correct(on_basis, to_left, scale, gain, cols_v, cols_w, cols_s):
    count = to_left.shape[0]
    mixed = mm(on_basis, cols_v)
    part = lambda k: mixed[k * count : (k + 1) * count]
    basis = part(0)
    residual = part(1) + mm(to_left, cols_w)
    correction = scale * residual
    for m in range(INNER - 1):
        correction = scale * (residual + cols_s * correction - part(2 + m))
    return basis + gain * correction


def selected(table, target_count, count):
    rows = lax.broadcasted_iota(jnp.int32, (count, 1), 0)
    chosen = jnp.zeros((count, 1), f32)
    for t in range(target_count):
        chosen = jnp.where(rows == table.target(t), 1.0, chosen)
    return chosen


class Table:
    def __init__(self, ref, row_count, tile_count, target_count):
        self.ref, self.ends = ref, []
        at = 0
        for length in (row_count, tile_count, tile_count, target_count, 1):
            self.ends.append(at)
            at += length

    def seg(self, i):
        return self.ref[self.ends[0] + i]

    def owner(self, i):
        return self.ref[self.ends[1] + i]

    def row(self, i):
        return self.ref[self.ends[2] + i]

    def target(self, i):
        return self.ref[self.ends[3] + i]

    def col(self):
        return self.ref[self.ends[4]]


def apply_tiles(tiles, table, source, image, size):
    count = tiles.shape[0]
    image[...] = jnp.zeros_like(image)

    def step(n, carry):
        image[:, seg_slice(table.row(n), size)] += mm3(source(table.owner(n)), tiles[n])
        return carry

    lax.fori_loop(0, count, step, 0, unroll=8)


def apply_back(tiles, table, image, send, vectors, size):
    count = tiles.shape[0]

    def step(n, carry):
        picked = image[:vectors, seg_slice(table.row(n), size)]
        send[table.owner(n), :vectors, :] += mm3(picked, tiles[n])
        return carry

    lax.fori_loop(0, count, step, 0, unroll=8)


def pack_kernel(dims, table, tiles, vectors, send):
    table = Table(table, *dims)
    size = tiles.shape[-1]
    count = vectors.shape[0]
    group = size // count
    rows = count // group
    gram_v = mt(vectors[...], vectors[...])
    packed = lanes([gram_v[k * rows : (k + 1) * rows] for k in range(group)])
    for r in range(send.shape[0]):
        send[r, :count, :] = vectors[:, seg_slice(table.seg(r), size)]
        send[r, count : count + rows, :] = packed
    send[:, count + rows :, :] = jnp.zeros((send.shape[0], PAD, size), f32)

    def step(n, carry):
        tile = tiles[n]
        at = slice(count + rows, count + rows + 1)
        send[table.owner(n), at, :] += jnp.sum(tile * tile, axis=0, keepdims=True)
        return carry

    lax.fori_loop(0, tiles.shape[0], step, 0, unroll=8)


def turn_kernel(tiles, turned):
    def step(n, carry):
        turned[n] = tiles[n].T
        return carry

    lax.fori_loop(0, tiles.shape[0], step, 0, unroll=4)


def unpack(packed, count):
    return jnp.concatenate(
        [packed[:, k * count : (k + 1) * count] for k in range(packed.shape[1] // count)], axis=0
    )


def first_kernel(dims, table, turned, got, image, squares):
    table = Table(table, *dims)
    size = turned.shape[-1]
    count = image.shape[0]
    rows = got.shape[1] - count - PAD
    span = image.shape[1] - size
    squares[...] = jnp.zeros_like(squares)
    packed = got[0, count : count + rows, :]
    for r in range(got.shape[0]):
        squares[:, seg_slice(table.seg(r), size)] += got[r, count + rows :, :]
        if r:
            packed = packed + got[r, count : count + rows, :]
    apply_tiles(turned, table, lambda o: got[o, :count, :], image, size)
    image[:, span : span + count] = unpack(packed, count)
    where = lax.broadcasted_iota(jnp.int32, (count, size - count), 1) == table.col()
    image[:, span + count :] = jnp.where(where, jnp.max(squares[...]), 0.0)


def first_back_kernel(dims, parts_count, table, tiles, *refs):
    table = Table(table, *dims)
    parts, (send, gram_v, image) = refs[:parts_count], refs[parts_count:]
    size = tiles.shape[-1]
    count = image.shape[0]
    span = image.shape[1] - size
    image[...] = functools.reduce(jnp.add, [p[...] for p in parts])
    top = jnp.max(image[:, span + count :])
    gram_v[...] = image[:, span:]
    gram_y = mt(image[:, :span], image[:, :span])
    corner = (lax.broadcasted_iota(jnp.int32, (count, count), 0) == 0) & (
        lax.broadcasted_iota(jnp.int32, (count, count), 1) == count - 1
    )
    gram_y = jnp.where(corner, top, gram_y)
    group = size // count
    rows = count // group
    packed = lanes([gram_y[k * rows : (k + 1) * rows] for k in range(group)])
    send[:, :count, :] = jnp.zeros((send.shape[0], count, size), f32)
    for r in range(send.shape[0]):
        send[r, count:, :] = packed
    apply_back(tiles, table, image, send, count, size)


def first_factor_kernel(total_rows, gram_v, lower_inv):
    count = gram_v.shape[0]
    lower_inv[...] = factor_inverse(gram_v[:, :count] / total_rows)[1]


def powers_of(values, scales):
    powers = [values]
    for _ in range(INNER - 1):
        powers.append(powers[-1] * scales)
    return powers


def gather_cols(got, table, cols, count, size):
    cols[...] = jnp.zeros_like(cols)
    for r in range(got.shape[0]):
        cols[:, seg_slice(table.seg(r), size)] += got[r, :count, :]


def moment_kernel(dims, table, got, vectors, squares, send, moments, small, own_w, own_s):
    table = Table(table, *dims)
    count = vectors.shape[0]
    size = got.shape[-1]
    group = size // count
    gather_cols(got, table, own_w, count, size)
    extra = got[0, count:, :]
    top = extra
    for r in range(1, got.shape[0]):
        extra = extra + got[r, count:, :]
        top = jnp.maximum(top, got[r, count:, :])
    first_row = unpack(top, count)[0:1, count - 1 : count]
    own_s[...] = squares[...] / first_row
    gram_y = unpack(extra, count)
    corner = (lax.broadcasted_iota(jnp.int32, (count, count), 0) == 0) & (
        lax.broadcasted_iota(jnp.int32, (count, count), 1) == count - 1
    )
    gram_y = jnp.where(corner, gram_y[count - 1 : count, 0:1], gram_y)
    small[...] = lanes([gram_y] + [jnp.broadcast_to(first_row, (count, count))] * (group - 1))
    for r in range(send.shape[0]):
        at = seg_slice(table.seg(r), size)
        send[r, :count, :] = own_w[:, at]
        send[r, count:, :] = own_s[:, at]
    values = vectors[...]
    both = jnp.concatenate([values, own_w[...]], axis=0)
    scales = own_s[0:1, :]
    moments[...] = jnp.zeros_like(moments)
    for j in range(1, INNER):
        values = values * scales
        found = mt(both, values)
        moments[:, (j - 1) * count : j * count] = found[:count]
        moments[:, size + (j - 1) * count : size + j * count] = found[count:]


def factor_kernel(total_rows, small, first_inv, facts):
    count = small.shape[0]
    lower_inv, upper, to_left, scale = factor(
        first_inv[...], small[:, :count], small[0:1, count : count + 1], total_rows
    )
    facts[0] = lower_inv
    facts[1] = upper
    facts[2] = to_left
    facts[3] = jnp.broadcast_to(scale, (count, count))


def second_kernel(
    dims, total_rows, parts_count, table, turned, got_v, got, vectors, own_w, own_s, small, facts, *refs
):
    table = Table(table, *dims)
    parts = refs[:parts_count]
    image, own_next, powers = refs[parts_count:]
    count = vectors.shape[0]
    size = turned.shape[-1]
    span = image.shape[1] - size
    moments = functools.reduce(jnp.add, [p[...] for p in parts])
    moments_vv = [moments[:, k * count : (k + 1) * count] for k in range(INNER - 1)]
    moments_wv = [moments[:, size + k * count : size + (k + 1) * count] for k in range(INNER - 1)]
    to_left, scale = facts[2], facts[3][:, 0:1]
    on_basis = couple((facts[0], facts[1], to_left, scale), moments_vv, moments_wv, total_rows)
    gain = selected(table, dims[2], count) / small[:, count : count + 1]
    tile_v = lanes([got_v[r, :count, :] for r in range(got.shape[0])])
    tile_w = lanes([got[r, :count, :] for r in range(got.shape[0])])
    tile_s = lanes([got[r, count : count + 1, :] for r in range(got.shape[0])])
    tile_v = correct(on_basis, to_left, scale, gain, tile_v, tile_w, tile_s)
    for k in range(INNER):
        for r in range(got.shape[0]):
            powers[r, k * count : (k + 1) * count, :] = tile_v[:, r * size : (r + 1) * size]
        if k + 1 < INNER:
            tile_v = tile_v * tile_s
    own = correct(on_basis, to_left, scale, gain, vectors[...], own_w[...], own_s[0:1, :])
    own_next[...] = own
    apply_tiles(turned, table, lambda o: powers[o], image, size)
    values = own
    for k in range(INNER):
        image[:count, span + k * count : span + (k + 1) * count] = mt(own, values)
        values = values * own_s[0:1, :]


def second_back_kernel(dims, parts_count, table, tiles, *refs):
    table = Table(table, *dims)
    parts, (send, moments, own_image, image) = refs[:parts_count], refs[parts_count:]
    size = tiles.shape[-1]
    count, width = own_image.shape
    span = image.shape[1]
    image[...] = functools.reduce(jnp.add, [p[:count, :span] for p in parts])
    moments[:, :size] = functools.reduce(jnp.add, [p[:count, span:] for p in parts])
    others = functools.reduce(jnp.add, [p[:, :span] for p in parts])
    moments[:, size:] = mt(image[...], others)
    own_image[...] = image[:, pl.ds(pl.multiple_of(table.col() * width, width), width)]
    send[...] = jnp.zeros_like(send)
    apply_back(tiles, table, image, send, count, size)


def second_factor_kernel(total_rows, parts_count, small, *refs):
    parts, (facts, triangle, on_basis) = refs[:parts_count], refs[parts_count:]
    count = small.shape[0]
    moments = functools.reduce(jnp.add, [p[...] for p in parts])
    pick = lambda k: moments[:, k * count : (k + 1) * count]
    lower_inv = factor_inverse(pick(0) / total_rows)[1]
    found = factor(lower_inv, pick(INNER), small[0:1, count : count + 1], total_rows)
    triangle[...] = found[1]
    facts[0] = found[2]
    facts[1] = jnp.broadcast_to(found[3], (count, count))
    on_basis[...] = couple(
        found,
        [pick(k) for k in range(1, INNER)],
        [pick(INNER + k) for k in range(1, INNER)],
        total_rows,
    )


def trial_kernel(dims, table, got, vectors, own_s, small, facts, on_basis, trial, send, own_w):
    table = Table(table, *dims)
    count = vectors.shape[0]
    size = got.shape[-1]
    gather_cols(got, table, own_w, count, size)
    gain = selected(table, dims[2], count) / small[:, count : count + 1]
    found = correct(
        on_basis[...], facts[0], facts[1][:, 0:1], gain, vectors[...], own_w[...], own_s[0:1, :]
    )
    trial[...] = found
    gram_sum = mt(found, found)
    rows = send.shape[1]
    packed = lanes([gram_sum[k * rows : (k + 1) * rows] for k in range(count // rows)])
    for r in range(send.shape[0]):
        send[r] = packed


def last_kernel(total_rows, got, trial, image, facts, right, left):
    count = trial.shape[0]
    packed = got[0]
    for r in range(1, got.shape[0]):
        packed = packed + got[r]
    left[...] = mm(facts[0], image[...])
    lower_inv = factor_inverse(unpack(packed, count) / total_rows)[1]
    right[...] = mm(lower_inv, trial[...])


def shards(blocks, block_rows, block_cols, start_basis, targets):
    size = blocks.shape[-1]
    tiles = blocks.reshape(-1, size, size)
    rows = block_rows.reshape(-1)
    row_count = lax.axis_size("row")
    col_count = lax.axis_size("col")
    count, width = start_basis.shape
    seg_count = width // size
    span = col_count * width
    total_rows = float(width * row_count * col_count)
    pattern = block_cols[:, 0, :]
    me_row = lax.axis_index("row")
    me_col = lax.axis_index("col")
    owners = lax.dynamic_index_in_dim(pattern, me_row, 0, keepdims=False) // seg_count
    segs = jnp.max(jnp.where(pattern // seg_count == me_row, pattern % seg_count, 0), axis=1)
    table = jnp.concatenate([segs, owners, rows, targets, me_col.reshape(1)])
    dims = (row_count, tiles.shape[0], targets.shape[0])
    packed = count * count // size

    def run(kernel, outs, args, *settings, **named):
        kernel = functools.partial(kernel, *settings)
        return call(kernel, outs, args, **named)

    (send,) = run(
        pack_kernel,
        [(row_count, count + packed + PAD, size)],
        [table, tiles, start_basis],
        dims,
        name="pack",
    )
    got_v = exchange(send)
    (turned,) = run(turn_kernel, [tiles.shape], [tiles], name="turn")
    part, squares = run(
        first_kernel,
        [(count, span + size), (PAD, width)],
        [table, turned, got_v],
        dims,
        name="first",
    )
    parts = axis_parts(part, "col")
    send, gram_v = run(
        first_back_kernel,
        [(row_count, count + packed, size), (count, size)],
        [table, tiles] + parts,
        dims,
        len(parts),
        scratch=[pltpu.VMEM((count, span + size), f32)],
        name="first_back",
    )
    got = exchange(send)
    (first_inv,) = run(
        first_factor_kernel, [(count, count)], [gram_v], total_rows, name="first_factor"
    )
    send, moments, small, own_w, own_s = run(
        moment_kernel,
        [
            (row_count, count + PAD, size),
            (count, 2 * size),
            (count, size),
            (count, width),
            (PAD, width),
        ],
        [table, got, start_basis, squares],
        dims,
        name="moments",
    )
    got = exchange(send)
    parts = axis_parts(add(axis_parts(moments, "col")), "row")
    (facts,) = run(
        factor_kernel, [(4, count, count)], [small, first_inv], total_rows, name="factor"
    )
    part, own_v = run(
        second_kernel,
        [(INNER * count, span + size), (count, width)],
        [table, turned, got_v, got, start_basis, own_w, own_s, small, facts] + parts,
        dims,
        total_rows,
        len(parts),
        scratch=[pltpu.VMEM((row_count, INNER * count, size), f32)],
        name="second",
    )
    parts = axis_parts(part, "col")
    send, moments, image = run(
        second_back_kernel,
        [(row_count, count, size), (count, 2 * size), (count, width)],
        [table, tiles] + parts,
        dims,
        len(parts),
        scratch=[pltpu.VMEM((count, span), f32)],
        name="second_back",
    )
    got = exchange(send)
    parts = axis_parts(moments, "row")
    facts, triangle, on_basis = run(
        second_factor_kernel,
        [(2, count, count), (count, count), ((INNER + 1) * count, count)],
        [small] + parts,
        total_rows,
        len(parts),
        name="second_factor",
    )
    trial, send = run(
        trial_kernel,
        [(count, width), (row_count * col_count, packed, size)],
        [table, got, own_v, own_s, small, facts, on_basis],
        dims,
        scratch=[pltpu.VMEM((count, width), f32)],
        name="trial",
    )
    got = exchange(send, ("row", "col"))
    right, left = run(
        last_kernel,
        [(count, width), (count, width)],
        [got, trial, image, facts],
        total_rows,
        name="last",
    )
    return right, left, triangle


def solution(mesh):
    in_specs = (
        P("row", "col", None, None, None),
        P("row", "col", None),
        P(None, "col", None),
        P(None, ("row", "col")),
        P(),
    )
    out_specs = (P(None, ("row", "col")), P(None, ("row", "col")), P())
    return jax.shard_map(shards, mesh=mesh, in_specs=in_specs, out_specs=out_specs, check_vma=False)
```

```python
import functools
import math

import jax
import jax.numpy as jnp
from jax import lax
from jax.experimental import pallas as pl
from jax.experimental.pallas import tpu as pltpu
from jax.sharding import PartitionSpec as P

OUTER = 2
INNER = 4
PAD = 8
HINT = 1 << 31

highest = lax.Precision.HIGHEST
f32 = jnp.float32


def mm(a, b):
    return lax.dot_general(a, b, (((1,), (0,)), ((), ())), precision=highest, preferred_element_type=f32)


def mt(a, b):
    return lax.dot_general(a, b, (((1,), (1,)), ((), ())), precision=highest, preferred_element_type=f32)


def halves(x):
    high = x.astype(jnp.bfloat16)
    return high, (x - high.astype(f32)).astype(jnp.bfloat16)


def mm3(a, b):
    count = a.shape[0]
    a_high, a_low = halves(a)
    b_high, b_low = halves(b)
    dot = functools.partial(jnp.dot, preferred_element_type=f32)
    both = dot(jnp.concatenate([a_high, a_low], axis=0), b_high)
    return both[:count] + both[count:] + dot(a_high, b_low)


def lanes(values):
    return jnp.concatenate(values, axis=1)


def column(row):
    count = row.shape[1]
    eye = lax.broadcasted_iota(jnp.int32, (count, count), 0) == lax.broadcasted_iota(
        jnp.int32, (count, count), 1
    )
    return jnp.sum(jnp.where(eye, row, 0.0), axis=1, keepdims=True)


smem = pl.BlockSpec(memory_space=pltpu.SMEM)
vmem = pl.BlockSpec(memory_space=pltpu.VMEM)
hbm = pl.BlockSpec(memory_space=pltpu.HBM)


class Hbm:
    def __init__(self, value):
        self.value = value


def call(kernel, outs, args, scratch=(), name=None, cost=None):
    def spec(arg):
        if isinstance(arg, Hbm):
            return hbm
        return smem if jnp.issubdtype(arg.dtype, jnp.integer) else vmem

    def out_spec(out):
        return hbm if isinstance(out, Hbm) else smem if isinstance(out, int) else vmem

    def out_shape(out):
        if isinstance(out, int):
            return jax.ShapeDtypeStruct((out,), jnp.int32)
        return jax.ShapeDtypeStruct(out.value if isinstance(out, Hbm) else out, f32)

    estimate = None
    if cost is not None:
        estimate = pl.CostEstimate(flops=cost, bytes_accessed=0, transcendentals=0)
    return pl.pallas_call(
        kernel,
        out_shape=tuple(out_shape(o) for o in outs),
        in_specs=[spec(a) for a in args],
        out_specs=tuple(out_spec(o) for o in outs),
        scratch_shapes=list(scratch),
        compiler_params=pltpu.CompilerParams(vmem_limit_bytes=54_000_000),
        cost_estimate=estimate,
        name=name,
    )(*[a.value if isinstance(a, Hbm) else a for a in args])


def add_kernel(*refs):
    refs[-1][...] = functools.reduce(jnp.add, [p[...] for p in refs[:-1]])


def add(parts):
    if len(parts) == 1:
        return parts[0]
    return call(add_kernel, [parts[0].shape], parts, name="add")[0]


def axis_parts(x, axis):
    count = lax.axis_size(axis)
    if count & (count - 1):
        return [lax.psum(x, axis)]
    parts = [x]
    bit = 1
    while bit < count:
        x = add(parts)
        masks = (bit, 2 * bit, 3 * bit) if 2 * bit < count else (bit,)
        parts = [x] + [
            lax.ppermute(x, axis, [(i, i ^ mask) for i in range(count)]) for mask in masks
        ]
        bit *= 4
    return parts


def exchange(x, axes="row"):
    return lax.all_to_all(x, axes, split_axis=0, concat_axis=0, tiled=True)


def seg_slice(index, size):
    return pl.ds(pl.multiple_of(index * size, size), size)


def factor_inverse(gram_sum):
    count = gram_sum.shape[0]
    rows = lax.broadcasted_iota(jnp.int32, (count, count), 0)
    cols = lax.broadcasted_iota(jnp.int32, (count, count), 1)
    state = lanes([gram_sum, jnp.where(rows == cols, 1.0, 0.0)])
    below = lax.broadcasted_iota(jnp.int32, state.shape, 0)
    spread_col = lambda k: jnp.broadcast_to(state[:, k : k + 1], state.shape)
    current = spread_col(0)
    for k in range(count):
        ahead = spread_col(k + 1) if k + 1 < count else None
        factor = jnp.where(below > k, current, 0.0) * (1.0 / current[k : k + 1, :])
        if ahead is not None:
            ahead = ahead - factor * current[k + 1 : k + 2, :]
        state = state - factor * state[k : k + 1, :]
        current = ahead
    left = state[:, :count]
    diag = jnp.sum(jnp.where(rows == cols, left, 0.0), axis=1, keepdims=True)
    state = state * (1.0 / jnp.sqrt(diag))
    return jnp.where(cols >= rows, state[:, :count], 0.0), state[:, count:]


def factor(lower_inv, gram_y, top, total_rows):
    gram_image = mt(mm(lower_inv, gram_y / total_rows), lower_inv)
    upper, image_inv = factor_inverse(gram_image)
    sums = jnp.sum(upper * upper, axis=0, keepdims=True)
    scale = column(top / (sums + top))
    return lower_inv, upper, mm(image_inv, lower_inv), scale


def couple(facts, moments_vv, moments_wv, total_rows):
    lower_inv, upper, to_left, scale = facts
    bb = [mt(mm(lower_inv, m / total_rows), lower_inv) for m in moments_vv]
    rb = [
        mt(mm(to_left, m / total_rows), lower_inv) - mm(upper, b)
        for m, b in zip(moments_wv, bb)
    ]
    powers = [scale]
    for _ in range(INNER - 2):
        powers.append(powers[-1] * scale)
    couplings = []
    base = 0.0
    for m in range(INNER - 1):
        base = base + powers[m] * rb[m]
        value = base
        for k in range(m):
            value = value - powers[k] * mm(couplings[m - 1 - k], bb[k])
        couplings.append(value)
    on_basis = [lower_inv, -mm(upper, lower_inv)] + [mm(c, lower_inv) for c in couplings]
    return jnp.concatenate(on_basis, axis=0)


def correct(on_basis, to_left, scale, gain, cols_v, cols_w, cols_s):
    count = to_left.shape[0]
    mixed = mm(on_basis, cols_v)
    part = lambda k: mixed[k * count : (k + 1) * count]
    basis = part(0)
    residual = part(1) + mm(to_left, cols_w)
    correction = scale * residual
    for m in range(INNER - 1):
        correction = scale * (residual + cols_s * correction - part(2 + m))
    return basis + gain * correction


def selected(table, target_count, count):
    rows = lax.broadcasted_iota(jnp.int32, (count, 1), 0)
    chosen = jnp.zeros((count, 1), f32)
    for t in range(target_count):
        chosen = jnp.where(rows == table.target(t), 1.0, chosen)
    return chosen


class Table:
    def __init__(self, ref, row_count, tile_count, target_count):
        self.ref, self.ends = ref, []
        at = 0
        for length in (row_count, tile_count, tile_count, target_count):
            self.ends.append(at)
            at += length

    def seg(self, i):
        return self.ref[self.ends[0] + i]

    def owner(self, i):
        return self.ref[self.ends[1] + i]

    def row(self, i):
        return self.ref[self.ends[2] + i]

    def target(self, i):
        return self.ref[self.ends[3] + i]


class Tiles:
    def __init__(self, source, held, sems):
        self.source, self.held, self.sems = source, held, sems
        self.chunk = held.shape[0] // sems.shape[0]
        self.count = sems.shape[0]

    def copy(self, c):
        part = pl.ds(c * self.chunk, self.chunk)
        return pltpu.make_async_copy(self.source.at[part], self.held.at[part], self.sems.at[c])

    def start(self):
        for c in range(self.count):
            self.copy(c).start()

    def each(self, visit, carry=0):
        def step(c, carry):
            self.copy(c).wait()
            for k in range(self.chunk):
                n = c * self.chunk + k
                carry = visit(n, self.held[n], carry)
            return carry

        return lax.fori_loop(0, self.count, step, carry)


def tile_scratch(shape):
    chunk = math.gcd(shape[0], 8)
    return [pltpu.VMEM(shape, f32), pltpu.SemaphoreType.DMA((shape[0] // chunk,))]


def apply_tiles(tiles, table, source, image, size):
    image[...] = jnp.zeros_like(image)

    def visit(n, tile, carry):
        image[:, seg_slice(table.row(n), size)] += mm3(source(table.owner(n)), tile)
        return carry

    tiles.each(visit)


def apply_back(tiles, table, image, send, size):
    count = image.shape[0]

    def visit(n, tile, carry):
        picked = image[:, seg_slice(table.row(n), size)]
        send[table.owner(n), :count, :] += mm3(picked, tile)
        return carry

    tiles.each(visit)


def pack_kernel(seg_count, pattern, rows, targets, tile_source, vectors, send, table, *scratch):
    tiles = Tiles(tile_source, *scratch)
    tiles.start()
    me = lax.axis_index("row")
    row_count, tile_count = pattern.shape
    size = tile_source.shape[-1]
    count = vectors.shape[0]
    group = size // count
    high = count // group
    gram_v = mt(vectors[...], vectors[...])
    packed = lanes([gram_v[k * high : (k + 1) * high] for k in range(group)])
    for r in range(row_count):
        send[r, count : count + high, :] = packed
    send[:, count + high :, :] = jnp.zeros((row_count, PAD, size), f32)
    at = slice(count + high, count + high + 1)

    def visit(n, tile, segs):
        owner = lax.div(pattern[me, n], seg_count)
        table[row_count + n] = owner
        table[row_count + tile_count + n] = rows[n]
        send[owner, at, :] += jnp.sum(tile * tile, axis=0, keepdims=True)
        found = []
        for r in range(row_count):
            value = pattern[r, n]
            mine = lax.div(value, seg_count) == me
            found.append(jnp.where(mine, lax.rem(value, seg_count), segs[r]))
        return tuple(found)

    segs = tiles.each(visit, (jnp.int32(0),) * row_count)
    for r in range(row_count):
        table[r] = segs[r]
        send[r, :count, :] = vectors[:, seg_slice(segs[r], size)]
    for t in range(targets.shape[0]):
        table[row_count + 2 * tile_count + t] = targets[t]


def turn_kernel(tile_source, turned, tiles, sems, stage, out_sems):
    tiles = Tiles(tile_source, tiles, sems)
    tiles.start()
    chunk = tiles.chunk

    def out(c):
        part = pl.ds(c * chunk, chunk)
        return pltpu.make_async_copy(stage.at[part], turned.at[part], out_sems.at[c])

    def visit(n, tile, carry):
        stage[n] = tile.T
        return carry

    tiles.each(visit)
    for c in range(tiles.count):
        out(c).start()
    for c in range(tiles.count):
        out(c).wait()


def unpack(packed, count):
    return jnp.concatenate(
        [packed[:, k * count : (k + 1) * count] for k in range(packed.shape[1] // count)], axis=0
    )


def first_kernel(dims, table, turned, got, image, squares, *scratch):
    table = Table(table, *dims)
    tiles = Tiles(turned, *scratch)
    tiles.start()
    size = turned.shape[-1]
    count = image.shape[0]
    rows = got.shape[1] - count - PAD
    span = image.shape[1] - size
    squares[...] = jnp.zeros_like(squares)
    packed = got[0, count : count + rows, :]
    for r in range(got.shape[0]):
        squares[:, seg_slice(table.seg(r), size)] += got[r, count + rows :, :]
        if r:
            packed = packed + got[r, count : count + rows, :]
    apply_tiles(tiles, table, lambda o: got[o, :count, :], image, size)
    image[:, span : span + count] = unpack(packed, count)
    where = lax.broadcasted_iota(jnp.int32, (count, size - count), 1) == lax.axis_index("col")
    image[:, span + count :] = jnp.where(where, jnp.max(squares[...]), 0.0)


def first_back_kernel(dims, parts_count, table, tile_source, *refs):
    table = Table(table, *dims)
    parts, (send, gram_v, image, *scratch) = refs[:parts_count], refs[parts_count:]
    tiles = Tiles(tile_source, *scratch)
    tiles.start()
    size = tile_source.shape[-1]
    count, span = image.shape
    image[...] = functools.reduce(jnp.add, [p[:, :span] for p in parts])
    extra = functools.reduce(jnp.add, [p[:, span:] for p in parts])
    top = jnp.max(extra[:, count:])
    gram_v[...] = extra
    gram_y = mt(image[...], image[...])
    corner = (lax.broadcasted_iota(jnp.int32, (count, count), 0) == 0) & (
        lax.broadcasted_iota(jnp.int32, (count, count), 1) == count - 1
    )
    gram_y = jnp.where(corner, top, gram_y)
    group = size // count
    rows = count // group
    packed = lanes([gram_y[k * rows : (k + 1) * rows] for k in range(group)])
    send[:, :count, :] = jnp.zeros((send.shape[0], count, size), f32)
    for r in range(send.shape[0]):
        send[r, count:, :] = packed
    apply_back(tiles, table, image, send, size)


def first_factor_kernel(total_rows, gram_v, lower_inv):
    count = gram_v.shape[0]
    lower_inv[...] = factor_inverse(gram_v[:, :count] / total_rows)[1]


def powers_of(values, scales):
    powers = [values]
    for _ in range(INNER - 1):
        powers.append(powers[-1] * scales)
    return powers


def gather_cols(got, table, cols, count, size):
    cols[...] = jnp.zeros_like(cols)
    for r in range(got.shape[0]):
        cols[:, seg_slice(table.seg(r), size)] += got[r, :count, :]


def moment_kernel(dims, table, got, vectors, squares, send, moments, small, own_w, own_s):
    table = Table(table, *dims)
    count = vectors.shape[0]
    size = got.shape[-1]
    group = size // count
    gather_cols(got, table, own_w, count, size)
    extra = got[0, count:, :]
    top = extra
    for r in range(1, got.shape[0]):
        extra = extra + got[r, count:, :]
        top = jnp.maximum(top, got[r, count:, :])
    first_row = unpack(top, count)[0:1, count - 1 : count]
    own_s[...] = squares[...] / first_row
    gram_y = unpack(extra, count)
    corner = (lax.broadcasted_iota(jnp.int32, (count, count), 0) == 0) & (
        lax.broadcasted_iota(jnp.int32, (count, count), 1) == count - 1
    )
    gram_y = jnp.where(corner, gram_y[count - 1 : count, 0:1], gram_y)
    small[...] = lanes([gram_y] + [jnp.broadcast_to(first_row, (count, count))] * (group - 1))
    for r in range(send.shape[0]):
        at = seg_slice(table.seg(r), size)
        send[r, :count, :] = own_w[:, at]
        send[r, count:, :] = own_s[:, at]
    values = vectors[...]
    both = jnp.concatenate([values, own_w[...]], axis=0)
    scales = own_s[0:1, :]
    moments[...] = jnp.zeros_like(moments)
    for j in range(1, INNER):
        values = values * scales
        found = mt(both, values)
        moments[:, (j - 1) * count : j * count] = found[:count]
        moments[:, size + (j - 1) * count : size + j * count] = found[count:]


def factor_kernel(total_rows, small, first_inv, facts):
    count = small.shape[0]
    lower_inv, upper, to_left, scale = factor(
        first_inv[...], small[:, :count], small[0:1, count : count + 1], total_rows
    )
    facts[0] = lower_inv
    facts[1] = upper
    facts[2] = to_left
    facts[3] = jnp.broadcast_to(scale, (count, count))


def second_kernel(
    dims, total_rows, parts_count, table, turned, got_v, got, vectors, own_w, own_s, small, facts, *refs
):
    table = Table(table, *dims)
    parts = refs[:parts_count]
    image, own_next, powers, *scratch = refs[parts_count:]
    tiles = Tiles(turned, *scratch)
    tiles.start()
    count = vectors.shape[0]
    size = turned.shape[-1]
    span = image.shape[1] - size
    moments = functools.reduce(jnp.add, [p[...] for p in parts])
    moments_vv = [moments[:, k * count : (k + 1) * count] for k in range(INNER - 1)]
    moments_wv = [moments[:, size + k * count : size + (k + 1) * count] for k in range(INNER - 1)]
    to_left, scale = facts[2], facts[3][:, 0:1]
    on_basis = couple((facts[0], facts[1], to_left, scale), moments_vv, moments_wv, total_rows)
    gain = selected(table, dims[2], count) / small[:, count : count + 1]
    tile_v = lanes([got_v[r, :count, :] for r in range(got.shape[0])])
    tile_w = lanes([got[r, :count, :] for r in range(got.shape[0])])
    tile_s = lanes([got[r, count : count + 1, :] for r in range(got.shape[0])])
    tile_v = correct(on_basis, to_left, scale, gain, tile_v, tile_w, tile_s)
    for k in range(INNER):
        for r in range(got.shape[0]):
            powers[r, k * count : (k + 1) * count, :] = tile_v[:, r * size : (r + 1) * size]
        if k + 1 < INNER:
            tile_v = tile_v * tile_s
    own = correct(on_basis, to_left, scale, gain, vectors[...], own_w[...], own_s[0:1, :])
    own_next[...] = own
    apply_tiles(tiles, table, lambda o: powers[o], image, size)
    values = own
    for k in range(INNER):
        image[:count, span + k * count : span + (k + 1) * count] = mt(own, values)
        values = values * own_s[0:1, :]


def second_back_kernel(dims, parts_count, table, tile_source, *refs):
    table = Table(table, *dims)
    parts, (send, moments, own_image, image, *scratch) = refs[:parts_count], refs[parts_count:]
    tiles = Tiles(tile_source, *scratch)
    tiles.start()
    size = tile_source.shape[-1]
    count, width = own_image.shape
    span = image.shape[1]
    image[...] = functools.reduce(jnp.add, [p[:count, :span] for p in parts])
    moments[:, :size] = functools.reduce(jnp.add, [p[:count, span:] for p in parts])
    others = functools.reduce(jnp.add, [p[:, :span] for p in parts])
    moments[:, size:] = mt(image[...], others)
    own_image[...] = image[:, seg_slice(lax.axis_index("col"), width)]
    send[...] = jnp.zeros_like(send)
    apply_back(tiles, table, image, send, size)


def second_factor_kernel(total_rows, parts_count, small, *refs):
    parts, (facts, triangle, on_basis) = refs[:parts_count], refs[parts_count:]
    count = small.shape[0]
    moments = functools.reduce(jnp.add, [p[...] for p in parts])
    pick = lambda k: moments[:, k * count : (k + 1) * count]
    lower_inv = factor_inverse(pick(0) / total_rows)[1]
    found = factor(lower_inv, pick(INNER), small[0:1, count : count + 1], total_rows)
    triangle[...] = found[1]
    facts[0] = found[2]
    facts[1] = jnp.broadcast_to(found[3], (count, count))
    on_basis[...] = couple(
        found,
        [pick(k) for k in range(1, INNER)],
        [pick(INNER + k) for k in range(1, INNER)],
        total_rows,
    )


def trial_kernel(dims, table, got, vectors, own_s, small, facts, on_basis, trial, send, own_w):
    table = Table(table, *dims)
    count = vectors.shape[0]
    size = got.shape[-1]
    gather_cols(got, table, own_w, count, size)
    gain = selected(table, dims[2], count) / small[:, count : count + 1]
    found = correct(
        on_basis[...], facts[0], facts[1][:, 0:1], gain, vectors[...], own_w[...], own_s[0:1, :]
    )
    trial[...] = found
    gram_sum = mt(found, found)
    rows = send.shape[1]
    packed = lanes([gram_sum[k * rows : (k + 1) * rows] for k in range(count // rows)])
    for r in range(send.shape[0]):
        send[r] = packed


def last_kernel(total_rows, got, trial, image, facts, right, left):
    count = trial.shape[0]
    packed = got[0]
    for r in range(1, got.shape[0]):
        packed = packed + got[r]
    left[...] = mm(facts[0], image[...])
    lower_inv = factor_inverse(unpack(packed, count) / total_rows)[1]
    right[...] = mm(lower_inv, trial[...])


def shards(blocks, block_rows, block_cols, start_basis, targets):
    size = blocks.shape[-1]
    tiles = blocks.reshape(-1, size, size)
    rows = block_rows.reshape(-1)
    row_count = lax.axis_size("row")
    col_count = lax.axis_size("col")
    count, width = start_basis.shape
    seg_count = width // size
    span = col_count * width
    total_rows = float(width * row_count * col_count)
    pattern = block_cols[:, 0, :]
    dims = (row_count, tiles.shape[0], targets.shape[0])
    packed = count * count // size

    def run(kernel, outs, args, *settings, **named):
        kernel = functools.partial(kernel, *settings)
        return call(kernel, outs, args, **named)

    held = tile_scratch(tiles.shape)
    (send, table) = run(
        pack_kernel,
        [(row_count, count + packed + PAD, size), row_count + 2 * dims[1] + dims[2]],
        [pattern, rows, targets, Hbm(tiles), start_basis],
        seg_count,
        scratch=held,
        name="pack",
    )
    got_v = exchange(send)
    (turned,) = run(
        turn_kernel, [Hbm(tiles.shape)], [Hbm(tiles)], scratch=held + held, name="turn", cost=HINT
    )
    part, squares = run(
        first_kernel,
        [(count, span + size), (PAD, width)],
        [table, Hbm(turned), got_v],
        dims,
        scratch=held,
        name="first",
    )
    parts = axis_parts(part, "col")
    send, gram_v = run(
        first_back_kernel,
        [(row_count, count + packed, size), (count, size)],
        [table, Hbm(tiles)] + parts,
        dims,
        len(parts),
        scratch=[pltpu.VMEM((count, span), f32)] + held,
        name="first_back",
    )
    got = exchange(send)
    (first_inv,) = run(
        first_factor_kernel, [(count, count)], [gram_v], total_rows, name="first_factor", cost=HINT
    )
    send, moments, small, own_w, own_s = run(
        moment_kernel,
        [
            (row_count, count + PAD, size),
            (count, 2 * size),
            (count, size),
            (count, width),
            (PAD, width),
        ],
        [table, got, start_basis, squares],
        dims,
        name="moments",
    )
    got = exchange(send)
    parts = axis_parts(add(axis_parts(moments, "col")), "row")
    (facts,) = run(
        factor_kernel, [(4, count, count)], [small, first_inv], total_rows, name="factor", cost=HINT
    )
    part, own_v = run(
        second_kernel,
        [(INNER * count, span + size), (count, width)],
        [table, Hbm(turned), got_v, got, start_basis, own_w, own_s, small, facts] + parts,
        dims,
        total_rows,
        len(parts),
        scratch=[pltpu.VMEM((row_count, INNER * count, size), f32)] + held,
        name="second",
    )
    parts = axis_parts(part, "col")
    send, moments, image = run(
        second_back_kernel,
        [(row_count, count, size), (count, 2 * size), (count, width)],
        [table, Hbm(tiles)] + parts,
        dims,
        len(parts),
        scratch=[pltpu.VMEM((count, span), f32)] + held,
        name="second_back",
    )
    got = exchange(send)
    parts = axis_parts(moments, "row")
    facts, triangle, on_basis = run(
        second_factor_kernel,
        [(2, count, count), (count, count), ((INNER + 1) * count, count)],
        [small] + parts,
        total_rows,
        len(parts),
        name="second_factor",
    )
    trial, send = run(
        trial_kernel,
        [(count, width), (row_count * col_count, packed, size)],
        [table, got, own_v, own_s, small, facts, on_basis],
        dims,
        scratch=[pltpu.VMEM((count, width), f32)],
        name="trial",
    )
    got = exchange(send, ("row", "col"))
    right, left = run(
        last_kernel,
        [(count, width), (count, width)],
        [got, trial, image, facts],
        total_rows,
        name="last",
    )
    return right, left, triangle


def solution(mesh):
    in_specs = (
        P("row", "col", None, None, None),
        P("row", "col", None),
        P(None, "col", None),
        P(None, ("row", "col")),
        P(),
    )
    out_specs = (P(None, ("row", "col")), P(None, ("row", "col")), P())
    return jax.shard_map(shards, mesh=mesh, in_specs=in_specs, out_specs=out_specs, check_vma=False)
```
